32 devices in a mesh: groups: 2 (over y), block: 4 (over x, core), tensor: 4 (over z).
Axes of the slice: x: 2, y: 2, z: 4, core: 2. Of those that a mesh axis runs over, the one named last changes fastest.
Arguments:
- tokens: bfloat16 [4096, 5120], P(('groups', 'block', 'tensor')), parts along dimension 0, may hold values from -20 to 20
- mod_shift: float32 [5120], replicated, may hold values from -3 to 3
- mod_scale: float32 [5120], replicated, may hold values from -0.5 to 0.5
- w_qkv: bfloat16 [3, 5120, 1024], P(None, 'block', 'tensor'), may hold values from -1 to 1
- tile_list: int32 [8, 4, 5], P(('groups', 'block')), parts along dimension 0, may hold values from 0 to 7, as said below
- tile_count: int32 [8, 4], P(('groups', 'block')), parts along dimension 0, may hold values from 2 to 5, as said below
Outputs:
- attended: bfloat16 [4096, 1024], P(('groups', 'block'), 'tensor'), parts along dimension 0
The draws below stay inside these ranges and needn't reach their ends.
There are 2 independent parts, one for each index of `groups`. The reference program is written for one: setup_inputs(seed, part) draws one part's arguments, and reference() takes and returns one part's arrays. A program takes and returns all parts, laid end to end along the dimension named above; an argument that names none is the same for every part. Nothing has to cross between parts.
Inputs may be any that keep to these rules, and one draw needn't show every extreme that they name: `tile_list`: within the first tile_count[c, t] slots the entries are distinct, the first is the query tile itself (2 + t), and none names a tile outside the slab; blocks at scene cuts name no tile of the block across the cut. Later slots hold indices in range and are not read. `tile_count`: the first query tile of every block reads 5 slots.
All inputs are finite; a program needn't handle non-finite values.
Results may differ from the reference program's by a relative error of at most 0.0087.
Values may be sent and summed in bfloat16 or wider, within the bound.
No kernel may reach another device: no remote copies, remote signals or barrier semaphores. Data moves between devices by JAX's collectives and lax.ppermute only.
A program may use at most 64 MiB of HBM per device.

```python
import jax
import jax.numpy as jnp
from jax import lax

D = 5120
HEAD_DIM = 128
BLOCK_TOK = 512
TILE = 128
BT = 2
KT = 5
HD = 1024
BLOCKS = 4
TOKENS = 2048
TPC = 4
NC = 8


def draw_tokens(key, part):
    first_key = jax.random.fold_in(key, 1)
    base = jax.random.normal(first_key, (TOKENS, D), jnp.float32)
    return jnp.clip(base, -20.0, 20.0).astype(jnp.bfloat16)


def draw_w_qkv(key, part):
    fan_scale = D ** (-0.5)
    noise = jax.random.normal(jax.random.fold_in(key, 5), (3, D, HD), jnp.float32) * fan_scale
    factors = jnp.array([1.5, 1.5, 1.0], jnp.float32)
    result = noise * factors[:, None, None]
    return jnp.clip(result, -1.0, 1.0).astype(jnp.bfloat16)


def tile_plan(key):
    cut_key = jax.random.fold_in(key, 11)
    score_key = jax.random.fold_in(key, 12)
    count_key = jax.random.fold_in(key, 13)
    block_ids = jnp.arange(BLOCKS, dtype=jnp.int32)
    cut_bits = jax.random.randint(cut_key, (BLOCKS,), 0, 2)
    cut_before = (cut_bits == 1) & (block_ids % 2 == 0) & (block_ids >= 2)
    cut_after = jnp.concatenate([cut_before[1:], jnp.zeros((1,), bool)])
    no_prev = (block_ids == 0) | cut_before
    no_next = (block_ids == BLOCKS - 1) | cut_after
    candidate = jnp.arange(NC, dtype=jnp.int32)
    valid = jnp.logical_not((candidate[None, :] < BT) & no_prev[:, None])
    valid = valid & jnp.logical_not((candidate[None, :] >= BT + TPC) & no_next[:, None])
    raw_scores = jax.random.randint(score_key, (BLOCKS, TPC, NC), 0, 1 << 20) * NC + candidate[None, None, :]
    own_tile = candidate[None, :] == (BT + jnp.arange(TPC, dtype=jnp.int32))[:, None]
    ranked = raw_scores + jnp.where(valid[:, None, :], 1 << 26, 0) + jnp.where(own_tile[None, :, :], 1 << 28, 0)
    unused, picked = lax.top_k(ranked, KT)
    counts = jax.random.randint(count_key, (BLOCKS, TPC), 2, KT + 1)
    tile_ids = jnp.arange(TPC, dtype=jnp.int32)[None, :]
    counts = jnp.where(tile_ids == 0, KT, counts)
    return (picked.astype(jnp.int32), counts.astype(jnp.int32))


def draw_tile_list(key, part):
    return tile_plan(key)[0]


def draw_tile_count(key, part):
    return tile_plan(key)[1]


def normal_values(stream_key, shape, deviation, most, kind=jnp.bfloat16):
    return jnp.clip(deviation * jax.random.normal(stream_key, shape, jnp.float32), -most, most).astype(kind)


def setup_inputs(seed: int = 0, part: int = 0) -> dict:
    key_of = jax.random.split(jax.random.key(seed), 7)
    part_keys = jax.random.split(jax.random.fold_in(key_of[6], part), 7)
    tokens = draw_tokens(jax.random.fold_in(jax.random.fold_in(key_of[6], part), 71), part)
    mod_shift = normal_values(key_of[1], (D,), 0.5, 3.0, jnp.float32)
    mod_scale = jnp.clip(jax.random.uniform(key_of[2], (D,), jnp.float32, -0.5, 0.5), -0.5, 0.5)
    w_qkv = draw_w_qkv(jax.random.fold_in(key_of[6], 71), part)
    tile_list = draw_tile_list(jax.random.fold_in(jax.random.fold_in(key_of[6], part), 71), part)
    tile_count = draw_tile_count(jax.random.fold_in(jax.random.fold_in(key_of[6], part), 71), part)
    return dict(tokens=tokens, mod_shift=mod_shift, mod_scale=mod_scale, w_qkv=w_qkv, tile_list=tile_list, tile_count=tile_count)


epsilon = 1e-06

def attend(queries, key_rows, value_rows, chosen_list, chosen_count):
    head_count = queries.shape[1] // HEAD_DIM
    local_tiles = queries.shape[0] // TILE
    all_tiles = key_rows.shape[0] // TILE
    slot_count = chosen_list.shape[1]
    shaped_queries = queries.reshape(local_tiles, TILE, head_count, HEAD_DIM).astype(jnp.float32)
    key_tiles = key_rows.reshape(all_tiles, TILE, head_count, HEAD_DIM)[chosen_list].astype(jnp.float32)
    value_tiles = value_rows.reshape(all_tiles, TILE, head_count, HEAD_DIM)[chosen_list].astype(jnp.float32)
    scores = jnp.einsum('pthd,pkshd->phtks', shaped_queries, key_tiles) * HEAD_DIM ** (-0.5)
    live_slot = jnp.arange(slot_count, dtype=jnp.int32)[None, :] < chosen_count[:, None]
    scores = jnp.where(live_slot[:, None, None, :, None], scores, jnp.float32(-1e+30))
    highest = lax.optimization_barrier(jnp.max(scores, axis=(3, 4), keepdims=True))
    exponent = jnp.exp(scores - highest)
    denominator = lax.optimization_barrier(jnp.sum(exponent, axis=(3, 4), keepdims=True))
    attn_weights = (exponent / denominator).astype(jnp.bfloat16)
    mixed = jnp.einsum('phtks,pkshd->pthd', attn_weights.astype(jnp.float32), value_tiles)
    return mixed.astype(jnp.bfloat16).reshape(local_tiles * TILE, head_count * HEAD_DIM)

def reference(tokens, mod_shift, mod_scale, w_qkv, tile_list, tile_count):
    values_in = tokens.astype(jnp.float32)
    row_mean = lax.optimization_barrier(jnp.mean(values_in, axis=1, keepdims=True))
    centred = values_in - row_mean
    row_var = lax.optimization_barrier(jnp.mean(centred * centred, axis=1, keepdims=True))
    normed = (centred * lax.rsqrt(row_var + epsilon) * (1.0 + mod_scale) + mod_shift).astype(jnp.bfloat16)
    queries = jnp.dot(normed, w_qkv[0], preferred_element_type=jnp.float32).astype(jnp.bfloat16)
    keys_all = jnp.dot(normed, w_qkv[1], preferred_element_type=jnp.float32).astype(jnp.bfloat16)
    values_all = jnp.dot(normed, w_qkv[2], preferred_element_type=jnp.float32).astype(jnp.bfloat16)
    margin = BT * TILE
    padding = jnp.zeros((margin, HD), jnp.bfloat16)
    keys_padded = jnp.concatenate([padding, keys_all, padding], axis=0)
    values_padded = jnp.concatenate([padding, values_all, padding], axis=0)

    def one_part(block_id):
        offset = (block_id * BLOCK_TOK).astype(jnp.int32)
        key_rows = lax.dynamic_slice_in_dim(keys_padded, offset, BLOCK_TOK + 2 * margin, 0)
        value_rows = lax.dynamic_slice_in_dim(values_padded, offset, BLOCK_TOK + 2 * margin, 0)
        own_queries = lax.dynamic_slice_in_dim(queries, offset, BLOCK_TOK, 0)
        return attend(own_queries, key_rows, value_rows, tile_list[block_id], tile_count[block_id])
    outputs = lax.map(one_part, jnp.arange(BLOCKS, dtype=jnp.int32))
    return outputs.reshape(TOKENS, HD)
```

```python
import functools

import jax
import jax.numpy as jnp
from jax import lax
from jax.experimental import pallas as pl
from jax.experimental.pallas import tpu as pltpu
from jax.sharding import PartitionSpec as P

HEAD_DIM = 128
TILE = 128
BT = 2
epsilon = 1e-06


def with_halo(x, sides, width):
    for axis, dim in sides:
        count, length = (lax.axis_size(axis), x.shape[dim])
        up = [(i, (i + 1) % count) for i in range(count - 1)]
        down = [(j, i) for i, j in up]
        last = lax.slice_in_dim(x, length - width, length, axis=dim)
        first = lax.slice_in_dim(x, 0, width, axis=dim)
        before = lax.ppermute(last, axis, up)
        after = lax.ppermute(first, axis, down)
        x = jnp.concatenate([before, x, after], axis=dim)
    return x


def attend(queries, key_rows, value_rows, chosen_list, chosen_count):
    head_count = queries.shape[1] // HEAD_DIM
    local_tiles = queries.shape[0] // TILE
    all_tiles = key_rows.shape[0] // TILE
    slot_count = chosen_list.shape[1]
    shaped_queries = queries.reshape(local_tiles, TILE, head_count, HEAD_DIM)
    key_tiles = key_rows.reshape(all_tiles, TILE, head_count, HEAD_DIM)[chosen_list]
    value_tiles = value_rows.reshape(all_tiles, TILE, head_count, HEAD_DIM)[chosen_list]
    scores = jnp.einsum(
        "pthd,pkshd->phtks", shaped_queries, key_tiles, preferred_element_type=jnp.float32
    )
    scores = scores * HEAD_DIM ** (-0.5)
    live_slot = jnp.arange(slot_count, dtype=jnp.int32)[None, :] < chosen_count[:, None]
    scores = jnp.where(live_slot[:, None, None, :, None], scores, jnp.float32(-1e30))
    highest = jnp.max(scores, axis=(3, 4), keepdims=True)
    exponent = jnp.exp(scores - highest)
    denominator = jnp.sum(exponent, axis=(3, 4), keepdims=True)
    attn_weights = (exponent / denominator).astype(jnp.bfloat16)
    mixed = jnp.einsum(
        "phtks,pkshd->pthd", attn_weights, value_tiles, preferred_element_type=jnp.float32
    )
    return mixed.astype(jnp.bfloat16).reshape(local_tiles * TILE, head_count * HEAD_DIM)


def general_shards(tokens, mod_shift, mod_scale, w_qkv, tile_list, tile_count):
    values_in = tokens.astype(jnp.float32)
    row_mean = jnp.mean(values_in, axis=1, keepdims=True)
    centred = values_in - row_mean
    row_var = jnp.mean(centred * centred, axis=1, keepdims=True)
    normed = (centred * lax.rsqrt(row_var + epsilon) * (1.0 + mod_scale) + mod_shift).astype(
        jnp.bfloat16
    )
    gathered = lax.all_gather(normed, "tensor", axis=0, tiled=True)
    projected = jnp.einsum(
        "td,ide->ite",
        gathered,
        lax.all_gather(w_qkv, "block", axis=1, tiled=True),
        preferred_element_type=jnp.float32,
    )
    projected = projected.astype(jnp.bfloat16)
    queries = projected[0]
    key_value = projected[1:3]
    extended = with_halo(key_value, (("block", 1),), BT * TILE)
    return attend(queries, extended[0], extended[1], tile_list[0], tile_count[0])


def ln_kernel(place_ref, x_ref, shift_ref, scale_ref, o_ref):
    quarters, _, depth = o_ref.shape
    x = x_ref[...].astype(jnp.float32)
    width = x.shape[1]
    mean = jnp.sum(x, axis=1, keepdims=True) * (1.0 / width)
    centred = x - mean
    var = jnp.sum(centred * centred, axis=1, keepdims=True) * (1.0 / width)
    rstd = lax.rsqrt(var + epsilon)
    normed = centred * rstd * (1.0 + scale_ref[...]) + shift_ref[...]
    normed = normed.astype(o_ref.dtype)
    for q in range(quarters):
        o_ref[jnp.bitwise_xor(place_ref[0], q)] = normed[:, q * depth : (q + 1) * depth]


def layer_norm(tokens, mod_shift, mod_scale, quarters):
    rows, width = tokens.shape
    depth = width // quarters
    step = 32
    place = lax.axis_index("block").astype(jnp.int32).reshape(1)
    return pl.pallas_call(
        ln_kernel,
        out_shape=jax.ShapeDtypeStruct((quarters, rows, depth), jnp.bfloat16),
        grid_spec=pltpu.PrefetchScalarGridSpec(
            num_scalar_prefetch=1,
            grid=(rows // step,),
            in_specs=[
                pl.BlockSpec((step, width), lambda i, p: (i, 0)),
                pl.BlockSpec((1, width), lambda i, p: (0, 0)),
                pl.BlockSpec((1, width), lambda i, p: (0, 0)),
            ],
            out_specs=pl.BlockSpec((quarters, step, depth), lambda i, p: (0, i, 0)),
        ),
        name="layer_norm",
    )(place, tokens, mod_shift.reshape(1, width), mod_scale.reshape(1, width))


def attn_kernel(list_ref, count_ref, tile_ref, y0, y1, y2, y3, near, far, o_ref, qb, kb, vb):
    tiles, slots = list_ref.shape
    width = o_ref.shape[1]
    for s, y in enumerate((y0, y1, y2, y3)):
        t = tile_ref[s]
        qb[t] = y[0]
        kb[BT + t] = y[1]
        vb[BT + t] = y[2]
    for h, ref in ((0, near), (1, far)):
        for i in range(BT):
            e = tile_ref[4 + 2 * h + i]
            kb[e] = ref[2 * i]
            vb[e] = ref[2 * i + 1]
    column = lax.broadcasted_iota(jnp.int32, (TILE, slots * TILE), 1)
    for t in range(tiles):
        live = column < count_ref[t] * TILE
        keys = [kb[list_ref[t, s]] for s in range(slots)]
        values = [vb[list_ref[t, s]] for s in range(slots)]
        for h in range(width // HEAD_DIM):
            head = slice(h * HEAD_DIM, (h + 1) * HEAD_DIM)
            q = qb[t][:, head]
            k = jnp.concatenate([key[:, head] for key in keys], axis=0)
            v = jnp.concatenate([value[:, head] for value in values], axis=0)
            scores = lax.dot_general(
                q, k, (((1,), (1,)), ((), ())), preferred_element_type=jnp.float32
            )
            scores = jnp.where(live, scores * HEAD_DIM ** (-0.5), jnp.float32(-1e30))
            highest = jnp.max(scores, axis=1, keepdims=True)
            exponent = jnp.exp(scores - highest)
            denominator = jnp.sum(exponent, axis=1, keepdims=True)
            weights = (exponent / denominator).astype(jnp.bfloat16)
            mixed = jnp.dot(weights, v, preferred_element_type=jnp.float32)
            o_ref[t * TILE : (t + 1) * TILE, head] = mixed.astype(o_ref.dtype)


def attention(chosen_list, chosen_count, tile_of, ys, near, far):
    tiles, slots = chosen_list.shape
    width = ys[0].shape[2]
    cands = tiles + 2 * BT
    vm = pl.BlockSpec(memory_space=pltpu.VMEM)
    sm = pl.BlockSpec(memory_space=pltpu.SMEM)
    return pl.pallas_call(
        attn_kernel,
        out_shape=jax.ShapeDtypeStruct((tiles * TILE, width), jnp.bfloat16),
        in_specs=[sm, sm, sm] + [vm] * 6,
        out_specs=vm,
        scratch_shapes=[
            pltpu.VMEM((tiles, TILE, width), jnp.bfloat16),
            pltpu.VMEM((cands, TILE, width), jnp.bfloat16),
            pltpu.VMEM((cands, TILE, width), jnp.bfloat16),
        ],
        name="attention",
    )(chosen_list, chosen_count, tile_of, *ys, near, far)


def line_shards(tokens, mod_shift, mod_scale, w_qkv, tile_list, tile_count):
    blocks, ranks = (lax.axis_size("block"), lax.axis_size("tensor"))
    both = ("block", "tensor")
    z = lax.axis_index("tensor")
    is_end = (z == 0) | (z == ranks - 1)

    def move(x, place):
        pairs = []
        for b in range(blocks):
            for r in range(ranks):
                to = place(b, r)
                if to is not None and 0 <= to[0] < blocks:
                    pairs.append((b * ranks + r, to[0] * ranks + to[1]))
        return lax.ppermute(x, both, pairs)

    pair = lambda x: move(x, lambda b, r: (b, r ^ 1))
    outward = lambda x: move(x, lambda b, r: (b, r ^ 1) if r in (1, 2) else None)
    middle = lambda x: move(x, lambda b, r: (b, 3 - r) if r in (1, 2) else None)
    sibling = lambda x: move(x, lambda b, r: (b ^ 1, r))
    across = lambda x: move(x, lambda b, r: (b ^ 2, r))
    near_halo = lambda x: move(x, lambda b, r: (b - 1, r) if r < 2 else (b + 1, r))
    far_halo = lambda x: move(x, lambda b, r: (b + 1, r) if r < 2 else (b - 1, r))

    w = [w_qkv, None, None, None]
    w[2] = across(w[0])
    w[1] = sibling(w[0])

    normed = layer_norm(tokens, mod_shift, mod_scale, blocks)
    own = [normed[0:2], normed[2:4]]
    partner = [pair(own[0]), pair(own[1])]
    mid = [middle(own[0]), middle(own[1])]
    far = [middle(partner[0]), middle(partner[1])]
    mid_out = [outward(mid[0]), outward(mid[1])]
    far_out = [outward(far[0]), outward(far[1])]
    mid = [jnp.where(is_end, o, i) for o, i in zip(mid_out, mid)]
    far = [jnp.where(is_end, o, i) for o, i in zip(far_out, far)]
    w[3] = sibling(w[2])

    def project(halves):
        total = None
        for h in range(2):
            for i in range(2):
                part = jnp.einsum(
                    "td,ide->ite", halves[h][i], w[2 * h + i], preferred_element_type=jnp.float32
                )
                total = part if total is None else total + part
        return total.astype(jnp.bfloat16)

    y0, y1, y2, y3 = (project(own), project(partner), project(mid), project(far))
    near = near_halo(jnp.concatenate([y0[1:3], y1[1:3]], axis=0))
    beyond = far_halo(jnp.concatenate([y2[1:3], y3[1:3]], axis=0))

    low = z < 2
    tiles = jnp.stack(
        [z, jnp.bitwise_xor(z, 1), jnp.where(low, 2, 1), jnp.where(low, 3, 0)]
    ).astype(jnp.int32)
    last = BT + tiles.shape[0]
    halo = jnp.where(low, last + tiles[0:2], tiles[0:2] - 2), jnp.where(
        low, tiles[2:4] - 2, last + tiles[2:4]
    )
    tile_of = jnp.concatenate([tiles, halo[0], halo[1]]).astype(jnp.int32)
    return attention(tile_list[0], tile_count[0], tile_of, (y0, y1, y2, y3), near, beyond)


def solution(mesh):
    on_line = mesh.shape["block"] == 4 and mesh.shape["tensor"] == 4
    return jax.shard_map(
        line_shards if on_line else general_shards,
        mesh=mesh,
        in_specs=(
            P(("groups", "block", "tensor"), None),
            P(),
            P(),
            P(None, "block", "tensor"),
            P(("groups", "block"), None, None),
            P(("groups", "block"), None),
        ),
        out_specs=P(("groups", "block"), "tensor"),
        check_vma=False,
    )
```
